32 devices in a mesh: ctx: 4 (over y, x), fsdp: 8 (over z, core).
Axes of the slice: x: 2, y: 2, z: 4, core: 2. Of those that a mesh axis runs over, the one named last changes fastest.
Arguments:
- hidden_in: bfloat16 [8, 1024, 1024], P('fsdp', 'ctx'), may hold values from -60 to 60
- lengths: int32 [8], P('fsdp'), may hold values from 128 to 1024, as said below
- block_of: int32 [8, 8], P('fsdp'), may hold values from 0 to 7, each once within a row
- qkv_weight: bfloat16 [1024, 3072], P('fsdp'), may hold values from -0.1875 to 0.1875
- qv_bias: bfloat16 [2048], P('fsdp'), may hold values from -3 to 3
- out_weight: bfloat16 [1024, 1024], P('fsdp'), may hold values from -1.5 to 1.5
- out_bias: bfloat16 [1024], P('fsdp'), may hold values from -3 to 3
- attn_gain: bfloat16 [1024], P('fsdp'), may hold values from 0.5 to 1.5
- attn_shift: bfloat16 [1024], P('fsdp'), may hold values from -3 to 3
- in_weight: bfloat16 [1024, 4096], P('fsdp'), may hold values from -0.1875 to 0.1875
- in_bias: bfloat16 [4096], P('fsdp'), may hold values from -3 to 3
- down_weight: bfloat16 [4096, 1024], P('fsdp'), may hold values from -0.09375 to 0.09375
- down_bias: bfloat16 [1024], P('fsdp'), may hold values from -3 to 3
- ffn_gain: bfloat16 [1024], P('fsdp'), may hold values from 0.5 to 1.5
- ffn_shift: bfloat16 [1024], P('fsdp'), may hold values from -3 to 3
- out_grad: bfloat16 [8, 1024, 1024], P('fsdp', 'ctx'), may hold values from -6 to 6
Outputs:
- hidden_out: bfloat16 [8, 1024, 1024], P('fsdp', 'ctx')
- in_grad: bfloat16 [8, 1024, 1024], P('fsdp', 'ctx')
- grad_qkv_weight: float32 [1024, 3072], P('fsdp')
- grad_qv_bias: float32 [2048], P('fsdp')
- grad_out_weight: float32 [1024, 1024], P('fsdp')
- grad_out_bias: float32 [1024], P('fsdp')
- grad_attn_gain: float32 [1024], P('fsdp')
- grad_attn_shift: float32 [1024], P('fsdp')
- grad_in_weight: float32 [1024, 4096], P('fsdp')
- grad_in_bias: float32 [4096], P('fsdp')
- grad_down_weight: float32 [4096, 1024], P('fsdp')
- grad_down_bias: float32 [1024], P('fsdp')
- grad_ffn_gain: float32 [1024], P('fsdp')
- grad_ffn_shift: float32 [1024], P('fsdp')
The draws below stay inside these ranges and needn't reach their ends.
Inputs may be any that keep to these rules, and one draw needn't show every extreme that they name: `lengths`: some sequence has length 1024 and some has length 128. `block_of`: each row names every block once.
All inputs are finite; a program needn't handle non-finite values.
Results may differ from the reference program's by a relative error of at most 0.013.
The reference program's roundings to bfloat16 on the way (of `mixed`, `inner_act`, `mixed_grad` and `score_grad`) count: a program that leaves them out, or rounds other values in their place, can miss the bound.
Values may be sent and summed in bfloat16 or wider, within the bound.
A program may use at most 256 MiB of HBM per device.

```python
import jax
import jax.numpy as jnp
from jax import lax

D = 1024
HEADS = 16
FF = 4096
SEQ = 1024
SEQS = 8
NBLK = 8


def draw_hidden_in(key, part):
    base_key = jax.random.fold_in(key, 0)
    values = jax.random.normal(base_key, (SEQS, SEQ, D), jnp.float32)
    return jnp.clip(values, -60.0, 60.0).astype(jnp.bfloat16)


def draw_lengths(key, part):
    pick_key, order_key = jax.random.split(key)
    length_draw = jax.random.randint(pick_key, (SEQS,), SEQ // 8, SEQ + 1, dtype=jnp.int32)
    ranking = jax.random.permutation(order_key, SEQS)
    length_draw = length_draw.at[ranking[0]].set(SEQ).at[ranking[1]].set(SEQ // 8)
    return length_draw


def block_scale(key, shape, shards, smallest, high):
    def one(axis_at, parts):
        steps = jax.random.uniform(jax.random.fold_in(jax.random.fold_in(key, 6), axis_at), (parts,), jnp.float32, smallest / len(shards), high / len(shards))
        return jnp.repeat(jnp.exp(steps), shape[axis_at] // parts).reshape((-1,) + (1,) * (len(shape) - axis_at - 1))

    level = one(*shards[0])
    for cut in shards[1:]:
        level = level * one(*cut)
    return level


def centred(stream_key, shape, scale, most, shards=(), held_as=jnp.bfloat16):
    entries = jax.random.normal(stream_key, shape, jnp.float32) * scale
    if len(shards) > 0:
        entries = block_scale(stream_key, shape, shards, -0.22, 0.18) * entries
    return jnp.clip(entries, min=-most, max=most).astype(held_as)


def setup_inputs(seed: int = 0) -> dict:
    splits = jax.random.split(jax.random.key(seed), 17)
    return {
        "hidden_in": draw_hidden_in(jax.random.fold_in(splits[16], 71), 0),
        "lengths": draw_lengths(jax.random.fold_in(splits[16], 71), 0),
        "block_of": jax.vmap(lambda own: jax.random.permutation(own, NBLK))(jax.random.split(splits[2], SEQS)).reshape((SEQS, NBLK)).astype(jnp.int32),
        "qkv_weight": centred(splits[3], (D, 3 * D), D ** -0.5, 0.1875, ((0, 8),)),
        "qv_bias": centred(splits[4], (2 * D,), 0.5, 3.0, ((0, 8),)),
        "out_weight": centred(splits[5], (D, D), (D * 16 // SEQ) ** -0.5, 1.5, ((0, 8),)),
        "out_bias": centred(splits[6], (D,), 0.5, 3.0, ((0, 8),)),
        "attn_gain": jnp.clip(1.0 + 0.1 * jax.random.normal(splits[7], (D,), jnp.float32), 0.5, 1.5).astype(jnp.bfloat16),
        "attn_shift": centred(splits[8], (D,), 0.5, 3.0, ((0, 8),)),
        "in_weight": centred(splits[9], (D, FF), D ** -0.5, 0.1875, ((0, 8),)),
        "in_bias": centred(splits[10], (FF,), 0.5, 3.0, ((0, 8),)),
        "down_weight": centred(splits[11], (FF, D), FF ** -0.5, 0.09375, ((0, 8),)),
        "down_bias": centred(splits[12], (D,), 0.5, 3.0, ((0, 8),)),
        "ffn_gain": jnp.clip(1.0 + 0.1 * jax.random.normal(splits[13], (D,), jnp.float32), 0.5, 1.5).astype(jnp.bfloat16),
        "ffn_shift": centred(splits[14], (D,), 0.5, 3.0, ((0, 8),)),
        "out_grad": centred(splits[15], (SEQS, SEQ, D), 1.0, 6.0, ((0, 8), (1, 4))),
    }


NEG_FILL = -1e+30
NORM_EPS = 1e-12
INV_ROOT_TWO = 0.7071067811865476
INV_ROOT_TAU = 0.3989422804014327

def split_heads(tensor):
    return tensor.reshape(tensor.shape[0], HEADS, -1)

def mix(pattern, left_op, right_op):
    return jnp.einsum(pattern, left_op.astype(jnp.float32), right_op.astype(jnp.float32))

def outer(left_op, right_op):
    return lax.dot_general(left_op, right_op, (((0,), (0,)), ((), ())), preferred_element_type=jnp.float32)

def against(left_op, right_op):
    return lax.dot_general(left_op, right_op, (((1,), (1,)), ((), ())), preferred_element_type=jnp.float32)

def key_valid(lengths, block_of, key_total):
    blocks = block_of.shape[1]
    block_size = key_total // blocks
    offsets = jnp.tile(jnp.arange(block_size, dtype=jnp.int32), blocks)
    places = jnp.repeat(block_of, block_size, axis=1) * block_size + offsets[None, :]
    return places < lengths[:, None]

def gelu_exact(values):
    return 0.5 * values * (1.0 + jax.scipy.special.erf(values * INV_ROOT_TWO))

def gelu_slope(values):
    return 0.5 * (1.0 + jax.scipy.special.erf(values * INV_ROOT_TWO)) + values * jnp.exp(-0.5 * values * values) * INV_ROOT_TAU

def layer_norm(values, gain_vec, shift_vec):
    center = values - lax.optimization_barrier(jnp.mean(values, axis=-1, keepdims=True))
    inv_scale = lax.rsqrt(lax.optimization_barrier(jnp.mean(center * center, axis=-1, keepdims=True)) + NORM_EPS)
    unit = center * inv_scale
    return (unit * gain_vec.astype(jnp.float32) + shift_vec.astype(jnp.float32), unit, inv_scale)

def norm_back(upstream, unit, inv_scale, gain_vec):
    scaled = upstream * gain_vec.astype(jnp.float32)
    return inv_scale * (scaled - lax.optimization_barrier(jnp.mean(scaled, axis=-1, keepdims=True)) - unit * lax.optimization_barrier(jnp.mean(scaled * unit, axis=-1, keepdims=True)))

def project(token_rows, qkv_weight, qv_bias):
    width = token_rows.shape[1]
    total = jnp.dot(token_rows, qkv_weight, preferred_element_type=jnp.float32)
    bias_full = qv_bias.astype(jnp.float32)
    queries = (total[:, :width] + bias_full[:width]).astype(jnp.bfloat16)
    keys_out = total[:, width:2 * width].astype(jnp.bfloat16)
    values_out = (total[:, 2 * width:] + bias_full[width:]).astype(jnp.bfloat16)
    return (queries, keys_out, values_out)

def score_block(query_one, key_one, allowed_one):
    score_scale = (query_one.shape[-1] // HEADS) ** (-0.5)
    scores = mix('qhd,khd->hqk', split_heads(query_one), split_heads(key_one)) * score_scale
    return jnp.where(allowed_one[None, None, :], scores, NEG_FILL)

def attend(query_seq, keys_all, values_all, allowed):

    def single(pieces):
        query_one, key_one, value_one, allowed_one = pieces
        scores = score_block(query_one, key_one, allowed_one)
        row_top = lax.optimization_barrier(jnp.max(scores, axis=-1, keepdims=True))
        log_total = row_top + jnp.log(lax.optimization_barrier(jnp.sum(jnp.exp(scores - row_top), axis=-1, keepdims=True)))
        probs_half = jnp.exp(scores - log_total).astype(jnp.bfloat16)
        mixed_out = mix('hqk,khd->qhd', probs_half, split_heads(value_one))
        return (mixed_out.reshape(mixed_out.shape[0], -1).astype(jnp.bfloat16), log_total[..., 0])
    return lax.map(single, (query_seq, keys_all, values_all, allowed))

def attend_back(query_seq, keys_all, values_all, allowed, log_totals, mixed_grad):

    def single(pieces):
        query_one, key_one, value_one, allowed_one, log_one, grad_one = pieces
        score_scale = (query_one.shape[-1] // HEADS) ** (-0.5)
        scores = score_block(query_one, key_one, allowed_one)
        probs = jnp.exp(scores - log_one[..., None])
        probs_half = probs.astype(jnp.bfloat16)
        value_grad = mix('hqk,qhd->khd', probs_half, split_heads(grad_one))
        prob_grad = mix('qhd,khd->hqk', split_heads(grad_one), split_heads(value_one))
        row_dot = lax.optimization_barrier(jnp.sum(probs * prob_grad, axis=-1, keepdims=True))
        score_grad = (probs * (prob_grad - row_dot) * score_scale).astype(jnp.bfloat16)
        query_grad = mix('hqk,khd->qhd', score_grad, split_heads(key_one))
        key_grad = mix('hqk,qhd->khd', score_grad, split_heads(query_one))
        return (query_grad.reshape(query_grad.shape[0], -1), key_grad.reshape(key_grad.shape[0], -1), value_grad.reshape(value_grad.shape[0], -1))
    return lax.map(single, (query_seq, keys_all, values_all, allowed, log_totals, mixed_grad))

def layer_pass(hidden_seq, cot_seq, allowed, params):
    qkv_weight, qv_bias, out_weight, out_bias, attn_gain, attn_shift, in_weight, in_bias, down_weight, down_bias, ffn_gain, ffn_shift = params
    seq_count, row_count, width = hidden_seq.shape
    token_rows = hidden_seq.reshape(seq_count * row_count, width)
    queries, keys_out, values_out = project(token_rows, qkv_weight, qv_bias)
    query_seq = queries.reshape(seq_count, row_count, width)
    keys_all = keys_out.reshape(seq_count, row_count, width)
    values_all = values_out.reshape(seq_count, row_count, width)
    mixed, log_totals = attend(query_seq, keys_all, values_all, allowed)
    mixed_rows = mixed.reshape(-1, width)
    attn_rows = jnp.dot(mixed_rows, out_weight, preferred_element_type=jnp.float32) + out_bias.astype(jnp.float32)
    first_sum = token_rows.astype(jnp.float32) + attn_rows
    first_norm, first_unit, first_scale = layer_norm(first_sum, attn_gain, attn_shift)
    first_half = first_norm.astype(jnp.bfloat16)
    inner_pre = jnp.dot(first_half, in_weight, preferred_element_type=jnp.float32) + in_bias.astype(jnp.float32)
    inner_act = gelu_exact(inner_pre).astype(jnp.bfloat16)
    second_sum = first_norm + jnp.dot(inner_act, down_weight, preferred_element_type=jnp.float32) + down_bias.astype(jnp.float32)
    result, second_unit, second_scale = layer_norm(second_sum, ffn_gain, ffn_shift)
    hidden_out = result.astype(jnp.bfloat16).reshape(seq_count, row_count, width)
    cot_rows = cot_seq.reshape(-1, width).astype(jnp.float32)
    grad_ffn_gain = lax.optimization_barrier(jnp.sum(cot_rows * second_unit, axis=0))
    grad_ffn_shift = lax.optimization_barrier(jnp.sum(cot_rows, axis=0))
    second_grad = norm_back(cot_rows, second_unit, second_scale, ffn_gain)
    second_half = second_grad.astype(jnp.bfloat16)
    grad_down_weight = outer(inner_act, second_half)
    grad_down_bias = lax.optimization_barrier(jnp.sum(second_grad, axis=0))
    inner_grad = against(second_half, down_weight) * gelu_slope(inner_pre)
    inner_half = inner_grad.astype(jnp.bfloat16)
    grad_in_weight = outer(first_half, inner_half)
    grad_in_bias = lax.optimization_barrier(jnp.sum(inner_grad, axis=0))
    first_back = second_grad + against(inner_half, in_weight)
    grad_attn_gain = lax.optimization_barrier(jnp.sum(first_back * first_unit, axis=0))
    grad_attn_shift = lax.optimization_barrier(jnp.sum(first_back, axis=0))
    first_grad = norm_back(first_back, first_unit, first_scale, attn_gain)
    attn_half = first_grad.astype(jnp.bfloat16)
    grad_out_weight = outer(mixed_rows, attn_half)
    grad_out_bias = lax.optimization_barrier(jnp.sum(first_grad, axis=0))
    mixed_grad = against(attn_half, out_weight).astype(jnp.bfloat16).reshape(seq_count, row_count, width)
    query_grad, key_grad, value_grad = attend_back(query_seq, keys_all, values_all, allowed, log_totals, mixed_grad)
    query_rows = query_grad.reshape(-1, width)
    value_rows = value_grad.reshape(-1, width)
    proj_half = jnp.concatenate([query_rows, key_grad.reshape(-1, width), value_rows], axis=1).astype(jnp.bfloat16)
    grad_qkv_weight = outer(token_rows, proj_half)
    grad_qv_bias = jnp.concatenate([lax.optimization_barrier(jnp.sum(query_rows, axis=0)), lax.optimization_barrier(jnp.sum(value_rows, axis=0))])
    in_grad = (first_grad + against(proj_half, qkv_weight)).astype(jnp.bfloat16).reshape(seq_count, row_count, width)
    grads = (grad_qkv_weight, grad_qv_bias, grad_out_weight, grad_out_bias, grad_attn_gain, grad_attn_shift, grad_in_weight, grad_in_bias, grad_down_weight, grad_down_bias, grad_ffn_gain, grad_ffn_shift)
    return (hidden_out, in_grad, grads)

def reference(hidden_in, lengths, block_of, qkv_weight, qv_bias, out_weight, out_bias, attn_gain, attn_shift, in_weight, in_bias, down_weight, down_bias, ffn_gain, ffn_shift, out_grad):
    params = (qkv_weight, qv_bias, out_weight, out_bias, attn_gain, attn_shift, in_weight, in_bias, down_weight, down_bias, ffn_gain, ffn_shift)
    allowed_all = key_valid(lengths, block_of, SEQ)
    grad_init = tuple((jnp.zeros(param_item.shape, jnp.float32) for param_item in params))

    def step(totals, inputs):
        seq_in, seq_cot, allowed_one = inputs
        result_out, result_grad, grads = layer_pass(seq_in[None], seq_cot[None], allowed_one[None], params)
        summed = tuple((total_item + grad_item for total_item, grad_item in zip(totals, grads)))
        return (summed, (result_out[0], result_grad[0]))
    totals, (outputs, input_grads) = lax.scan(step, grad_init, (hidden_in, out_grad, allowed_all))
    return (outputs, input_grads, totals[0], totals[1], totals[2], totals[3], totals[4], totals[5], totals[6], totals[7], totals[8], totals[9], totals[10], totals[11])
```

```python
import jax
import jax.numpy as jnp
from jax import lax
from jax.sharding import PartitionSpec as P

HEADS = 16


NEG_FILL = -1e30
NORM_EPS = 1e-12
INV_ROOT_TWO = 0.7071067811865476
INV_ROOT_TAU = 0.3989422804014327


def split_heads(tensor):
    return tensor.reshape(tensor.shape[0], HEADS, -1)


def mix(pattern, left_op, right_op):
    return jnp.einsum(pattern, left_op, right_op, preferred_element_type=jnp.float32)


def outer(left_op, right_op):
    return lax.dot_general(
        left_op, right_op, (((0,), (0,)), ((), ())), preferred_element_type=jnp.float32
    )


def against(left_op, right_op):
    return lax.dot_general(
        left_op, right_op, (((1,), (1,)), ((), ())), preferred_element_type=jnp.float32
    )


def key_valid(lengths, block_of, key_total):
    blocks = block_of.shape[1]
    block_size = key_total // blocks
    offsets = jnp.tile(jnp.arange(block_size, dtype=jnp.int32), blocks)
    places = jnp.repeat(block_of, block_size, axis=1) * block_size + offsets[None, :]
    return places < lengths[:, None]


def gelu_exact(values):
    return 0.5 * values * (1.0 + jax.scipy.special.erf(values * INV_ROOT_TWO))


def gelu_slope(values):
    return (
        0.5 * (1.0 + jax.scipy.special.erf(values * INV_ROOT_TWO))
        + values * jnp.exp(-0.5 * values * values) * INV_ROOT_TAU
    )


def layer_norm(values, gain_vec, shift_vec):
    center = values - jnp.mean(values, axis=-1, keepdims=True)
    inv_scale = lax.rsqrt(jnp.mean(center * center, axis=-1, keepdims=True) + NORM_EPS)
    unit = center * inv_scale
    return (unit * gain_vec.astype(jnp.float32) + shift_vec.astype(jnp.float32), unit, inv_scale)


def norm_back(upstream, unit, inv_scale, gain_vec):
    scaled = upstream * gain_vec.astype(jnp.float32)
    return inv_scale * (
        scaled
        - jnp.mean(scaled, axis=-1, keepdims=True)
        - unit * jnp.mean(scaled * unit, axis=-1, keepdims=True)
    )


def project(token_rows, qkv_full, bias_vec):
    width = token_rows.shape[1]
    total = jnp.dot(token_rows, qkv_full, preferred_element_type=jnp.float32)
    bias_full = bias_vec.astype(jnp.float32)
    queries = (total[:, :width] + bias_full[:width]).astype(jnp.bfloat16)
    keys_out = total[:, width : 2 * width].astype(jnp.bfloat16)
    values_out = (total[:, 2 * width :] + bias_full[width:]).astype(jnp.bfloat16)
    return (queries, keys_out, values_out)


def score_block(query_one, key_one, allowed_one):
    score_scale = (query_one.shape[-1] // HEADS) ** (-0.5)
    scores = mix("qhd,khd->hqk", split_heads(query_one), split_heads(key_one)) * score_scale
    return jnp.where(allowed_one[None, None, :], scores, NEG_FILL)


def attend(query_seq, keys_all, values_all, allowed):

    def single(pieces):
        query_one, key_one, value_one, allowed_one = pieces
        scores = score_block(query_one, key_one, allowed_one)
        row_top = jnp.max(scores, axis=-1, keepdims=True)
        log_total = row_top + jnp.log(jnp.sum(jnp.exp(scores - row_top), axis=-1, keepdims=True))
        probs_half = jnp.exp(scores - log_total).astype(jnp.bfloat16)
        mixed_out = mix("hqk,khd->qhd", probs_half, split_heads(value_one))
        return (mixed_out.reshape(mixed_out.shape[0], -1).astype(jnp.bfloat16), log_total[..., 0])

    return lax.map(single, (query_seq, keys_all, values_all, allowed))


def attend_back(query_seq, keys_all, values_all, allowed, log_totals, mixed_grad):

    def single(pieces):
        query_one, key_one, value_one, allowed_one, log_one, grad_one = pieces
        score_scale = (query_one.shape[-1] // HEADS) ** (-0.5)
        scores = score_block(query_one, key_one, allowed_one)
        probs = jnp.exp(scores - log_one[..., None])
        probs_half = probs.astype(jnp.bfloat16)
        value_grad = mix("hqk,qhd->khd", probs_half, split_heads(grad_one))
        prob_grad = mix("qhd,khd->hqk", split_heads(grad_one), split_heads(value_one))
        row_dot = jnp.sum(probs * prob_grad, axis=-1, keepdims=True)
        score_grad = (probs * (prob_grad - row_dot) * score_scale).astype(jnp.bfloat16)
        query_grad = mix("hqk,khd->qhd", score_grad, split_heads(key_one))
        key_grad = mix("hqk,qhd->khd", score_grad, split_heads(query_one))
        return (
            query_grad.reshape(query_grad.shape[0], -1),
            key_grad.reshape(key_grad.shape[0], -1),
            value_grad.reshape(value_grad.shape[0], -1),
        )

    return lax.map(single, (query_seq, keys_all, values_all, allowed, log_totals, mixed_grad))


def gather_smalls(smalls):
    packed = jnp.concatenate(smalls)[None]
    full = lax.all_gather(packed, "fsdp", axis=0, tiled=True)
    pieces = []
    at = 0
    for item in smalls:
        pieces.append(full[:, at : at + item.shape[0]].reshape(-1))
        at += item.shape[0]
    return pieces


def scatter_half(grad):
    return lax.psum_scatter(
        grad.astype(jnp.bfloat16), "fsdp", scatter_dimension=0, tiled=True
    )


def halve(values):
    return lax.reduce_precision(values, 8, 7).astype(jnp.bfloat16)


def swap_sum(part, order):
    size = lax.axis_size("ctx")
    for bit in order:
        other = lax.ppermute(part, "ctx", [(i, i ^ bit) for i in range(size)])
        total = part.astype(jnp.float32) + other.astype(jnp.float32)
        part = halve(total)
    return total


def sum_over_ctx(part):
    size = lax.axis_size("ctx")
    if size & (size - 1):
        return lax.psum(part.astype(jnp.float32), "ctx")
    order = [1 << k for k in range(size.bit_length() - 1)]
    mid = part.shape[0] // 2
    return jnp.concatenate(
        [swap_sum(part[:mid], order), swap_sum(part[mid:], order[::-1])], axis=0
    )


def local(
    hidden_in,
    lengths,
    block_of,
    qkv_weight,
    qv_bias,
    out_weight,
    out_bias,
    attn_gain,
    attn_shift,
    in_weight,
    in_bias,
    down_weight,
    down_bias,
    ffn_gain,
    ffn_shift,
    out_grad,
):
    seq_count, row_count, width = hidden_in.shape
    smalls = (qv_bias, out_bias, attn_gain, attn_shift, in_bias, down_bias, ffn_gain, ffn_shift)
    (
        full_qv_bias,
        full_out_bias,
        full_attn_gain,
        full_attn_shift,
        full_in_bias,
        full_down_bias,
        full_ffn_gain,
        full_ffn_shift,
    ) = gather_smalls(smalls)
    full_qkv = lax.all_gather(qkv_weight, "fsdp", axis=0, tiled=True)
    full_out_weight = lax.all_gather(out_weight, "fsdp", axis=0, tiled=True)
    full_in_weight = lax.all_gather(in_weight, "fsdp", axis=0, tiled=True)
    full_down_weight = lax.all_gather(down_weight, "fsdp", axis=0, tiled=True)
    token_rows = hidden_in.reshape(seq_count * row_count, width)
    queries, keys_local, values_local = project(token_rows, full_qkv, full_qv_bias)
    both_all = lax.all_gather(
        jnp.concatenate([keys_local, values_local], axis=1).reshape(
            seq_count, row_count, 2 * width
        ),
        "ctx",
        axis=1,
        tiled=True,
    )
    keys_all, values_all = both_all[..., :width], both_all[..., width:]
    allowed = key_valid(lengths, block_of, keys_all.shape[1])
    query_seq = queries.reshape(seq_count, row_count, width)
    mixed, log_totals = attend(query_seq, keys_all, values_all, allowed)
    mixed_rows = mixed.reshape(-1, width)
    attn_rows = jnp.dot(
        mixed_rows, full_out_weight, preferred_element_type=jnp.float32
    ) + full_out_bias.astype(jnp.float32)
    first_sum = token_rows.astype(jnp.float32) + attn_rows
    first_norm, first_unit, first_scale = layer_norm(first_sum, full_attn_gain, full_attn_shift)
    first_half = first_norm.astype(jnp.bfloat16)
    inner_pre = jnp.dot(
        first_half, full_in_weight, preferred_element_type=jnp.float32
    ) + full_in_bias.astype(jnp.float32)
    inner_act = gelu_exact(inner_pre).astype(jnp.bfloat16)
    second_sum = (
        first_norm
        + jnp.dot(inner_act, full_down_weight, preferred_element_type=jnp.float32)
        + full_down_bias.astype(jnp.float32)
    )
    result, second_unit, second_scale = layer_norm(second_sum, full_ffn_gain, full_ffn_shift)
    hidden_out = result.astype(jnp.bfloat16).reshape(seq_count, row_count, width)
    cot_rows = out_grad.reshape(-1, width).astype(jnp.float32)
    grad_ffn_gain = jnp.sum(cot_rows * second_unit, axis=0)
    grad_ffn_shift = jnp.sum(cot_rows, axis=0)
    second_grad = norm_back(cot_rows, second_unit, second_scale, full_ffn_gain)
    second_half = second_grad.astype(jnp.bfloat16)
    grad_down_weight = outer(inner_act, second_half)
    grad_down_bias = jnp.sum(second_grad, axis=0)
    inner_grad = against(second_half, full_down_weight) * gelu_slope(inner_pre)
    inner_half = inner_grad.astype(jnp.bfloat16)
    grad_in_weight = outer(first_half, inner_half)
    grad_in_bias = jnp.sum(inner_grad, axis=0)
    first_back = second_grad + against(inner_half, full_in_weight)
    grad_attn_gain = jnp.sum(first_back * first_unit, axis=0)
    grad_attn_shift = jnp.sum(first_back, axis=0)
    first_grad = norm_back(first_back, first_unit, first_scale, full_attn_gain)
    attn_half = first_grad.astype(jnp.bfloat16)
    grad_out_weight = outer(mixed_rows, attn_half)
    grad_out_bias = jnp.sum(first_grad, axis=0)
    mixed_grad = (
        against(attn_half, full_out_weight)
        .astype(jnp.bfloat16)
        .reshape(seq_count, row_count, width)
    )
    query_grad, key_grad, value_grad = attend_back(
        query_seq, keys_all, values_all, allowed, log_totals, mixed_grad
    )
    half_down = scatter_half(grad_down_weight)
    both_grad = jnp.concatenate([key_grad, value_grad], axis=2).astype(jnp.bfloat16)
    both_grad, half_down = lax.optimization_barrier((both_grad, half_down))
    both_own = lax.psum_scatter(both_grad, "ctx", scatter_dimension=1, tiled=True)
    half_in_grad, both_own = lax.optimization_barrier((grad_in_weight.astype(jnp.bfloat16), both_own))
    half_in = scatter_half(half_in_grad)
    key_own, value_own = both_own[..., :width], both_own[..., width:].astype(jnp.float32)
    query_rows = query_grad.reshape(-1, width)
    value_rows = value_own.reshape(-1, width)
    proj_half = jnp.concatenate(
        [query_rows.astype(jnp.bfloat16), key_own.reshape(-1, width), value_rows.astype(jnp.bfloat16)], axis=1
    ).astype(jnp.bfloat16)
    grad_qkv_weight = outer(token_rows, proj_half)
    grad_qv_bias = jnp.concatenate([jnp.sum(query_rows, axis=0), jnp.sum(value_rows, axis=0)])
    in_grad = (
        (first_grad + against(proj_half, full_qkv))
        .astype(jnp.bfloat16)
        .reshape(seq_count, row_count, width)
    )
    small_grads = (
        grad_qv_bias,
        grad_out_bias,
        grad_attn_gain,
        grad_attn_shift,
        grad_in_bias,
        grad_down_bias,
        grad_ffn_gain,
        grad_ffn_shift,
    )
    shards = lax.axis_size("fsdp")
    packed = jnp.concatenate([item.reshape(shards, -1) for item in small_grads], axis=1)
    extra = -(-packed.shape[1] // (16 * width)) * 16
    packed = jnp.pad(packed, ((0, 0), (0, extra * width - packed.shape[1])))
    own_rows = width // shards
    out_pack = jnp.concatenate(
        [
            grad_out_weight.reshape(shards, own_rows, width).astype(jnp.bfloat16),
            packed.reshape(shards, extra, width).astype(jnp.bfloat16),
        ],
        axis=1,
    ).reshape(shards * (own_rows + extra), width)
    half_qkv = scatter_half(grad_qkv_weight)
    out_pack, half_qkv = lax.optimization_barrier((out_pack, half_qkv))
    half_out = scatter_half(out_pack)
    total_down = sum_over_ctx(half_down)
    total_in = sum_over_ctx(half_in)
    total_qkv = sum_over_ctx(half_qkv)
    total_pack = sum_over_ctx(half_out)
    total_small = total_pack[own_rows:].reshape(-1)
    small_out = []
    at = 0
    for item in small_grads:
        size = item.shape[0] // shards
        small_out.append(total_small[at : at + size])
        at += size
    return (
        hidden_out,
        in_grad,
        total_qkv,
        small_out[0],
        total_pack[:own_rows],
        small_out[1],
        small_out[2],
        small_out[3],
        total_in,
        small_out[4],
        total_down,
        small_out[5],
        small_out[6],
        small_out[7],
    )


def solution(mesh):
    return jax.shard_map(
        local,
        mesh=mesh,
        in_specs=(
            P("fsdp", "ctx", None),
            P("fsdp"),
            P("fsdp", None),
            P("fsdp", None),
            P("fsdp"),
            P("fsdp", None),
            P("fsdp"),
            P("fsdp"),
            P("fsdp"),
            P("fsdp", None),
            P("fsdp"),
            P("fsdp", None),
            P("fsdp"),
            P("fsdp"),
            P("fsdp"),
            P("fsdp", "ctx", None),
        ),
        out_specs=(
            P("fsdp", "ctx", None),
            P("fsdp", "ctx", None),
            P("fsdp", None),
            P("fsdp"),
            P("fsdp", None),
            P("fsdp"),
            P("fsdp"),
            P("fsdp"),
            P("fsdp", None),
            P("fsdp"),
            P("fsdp", None),
            P("fsdp"),
            P("fsdp"),
            P("fsdp"),
        ),
        check_vma=False,
    )
```
